256 devices in a mesh: gx: 16 (over y, x), gy: 16 (over z, core).
Axes of the slice: x: 4, y: 4, z: 8, core: 2. Of those that a mesh axis runs over, the one named last changes fastest.
Arguments:
- source: float32 [128, 512, 256], P('gx', 'gy'), may hold values from -4 to 4
- damping: float32 [128, 512, 256], P('gx', 'gy'), may hold values from 0.0005 to 0.02
- coarse_one: float32 [27, 64, 256, 128], P(None, 'gx', 'gy'), may hold values from -1.5 to 22
- coarse_two: float32 [27, 32, 128, 64], P(None, 'gx', 'gy'), may hold values from -3 to 44
- coarse_three: float32 [27, 16, 64, 32], P(None, 'gx', 'gy'), may hold values from -6 to 87
Outputs:
- preconditioned: float32 [128, 512, 256], P('gx', 'gy')
The draws below stay inside these ranges and needn't reach their ends.
All inputs are finite; a program needn't handle non-finite values.
Results may differ from the reference program's by a relative error of at most 0.00008.
Values sent between devices are 32-bit elements; how exact they have to be, the bound alone decides.
No kernel may reach another device: no remote copies, remote signals or barrier semaphores. Data moves between devices by JAX's collectives and lax.ppermute only.
A program may use at most 64 MiB of HBM per device.

```python
import math
import jax
import jax.numpy as jnp
import numpy as np
from jax import lax

NZ = 256
NU = 4
CSWEEPS = 8
NX = 128
NY = 512


def stencil_draw(key, extent_x, extent_y, extent_z, strength):
    weights = np.array([0.0 if shift_x == 0 and shift_y == 0 and (shift_z == 0) else 0.5 ** (abs(shift_x) + abs(shift_y) + abs(shift_z)) for shift_x in (-1, 0, 1) for shift_y in (-1, 0, 1) for shift_z in (-1, 0, 1)], dtype=np.float32)
    factors = jax.random.uniform(jax.random.fold_in(key, 11), (27, extent_x, extent_y, extent_z), jnp.float32, 0.5, 1.5)
    off_diagonal = -strength * factors * jnp.asarray(weights)[:, None, None, None]
    surplus = jnp.exp(jax.random.uniform(jax.random.fold_in(key, 12), (extent_x, extent_y, extent_z), jnp.float32, math.log(0.001), math.log(0.03)))
    centre = jnp.sum(-off_diagonal, axis=0) * (1.0 + surplus)
    is_centre = (jnp.arange(27) == 13)[:, None, None, None]
    return jnp.where(is_centre, centre[None], off_diagonal).astype(jnp.float32)


def draw_source(key, part):
    values = jax.random.truncated_normal(jax.random.fold_in(key, 22), -4.0, 4.0, (NX, NY, NZ), jnp.float32)
    return values.astype(jnp.float32)


def draw_coarse_one(key, part):
    return stencil_draw(jax.random.fold_in(key, 31), NX // 2, NY // 2, NZ // 2, 2.0)


def draw_coarse_two(key, part):
    return stencil_draw(jax.random.fold_in(key, 32), NX // 4, NY // 4, NZ // 4, 4.0)


def draw_coarse_three(key, part):
    return stencil_draw(jax.random.fold_in(key, 33), NX // 8, NY // 8, NZ // 8, 8.0)


def steps_of(key, dims, split, low, top_value):
    level = 1.0
    for position, parts in split:
        steps = jax.random.uniform(jax.random.fold_in(jax.random.fold_in(key, 6), position), (parts,), jnp.float32, low / len(split), top_value / len(split))
        level = level * jnp.repeat(jnp.exp(steps), dims[position] // parts).reshape((-1,) + (1,) * (len(dims) - 1 - position))
    return level


def setup_inputs(seed: int = 0) -> dict:
    splits = jax.random.split(jax.random.key(seed), 6)
    return {
        "source": draw_source(jax.random.fold_in(splits[5], 71), 0),
        "damping": jnp.clip(jnp.exp(math.log(0.02) - 3.6888794 * jax.random.uniform(splits[1], (NX, NY, NZ), jnp.float32) ** steps_of(splits[1], (NX, NY, NZ), ((0, 16), (1, 16)), -0.2, 0.2)), 0.0005, 0.02),
        "coarse_one": draw_coarse_one(jax.random.fold_in(splits[5], 71), 0),
        "coarse_two": draw_coarse_two(jax.random.fold_in(splits[5], 71), 0),
        "coarse_three": draw_coarse_three(jax.random.fold_in(splits[5], 71), 0),
    }


RELAXATION = 0.8
OFFSETS = tuple((shift_x, shift_y, shift_z) for shift_x in (-1, 0, 1) for shift_y in (-1, 0, 1) for shift_z in (-1, 0, 1))


def pad_along(field, along_dim):
    widths = [(0, 0)] * field.ndim
    widths[along_dim] = (1, 1)
    return jnp.pad(field, widths)


def pad_plane(field):
    return jnp.pad(field, ((1, 1), (1, 1), (0, 0)))


def seven_point(extended, damping):
    extent_x, extent_y = damping.shape[0], damping.shape[1]
    padded = pad_along(extended, 2)
    centre = extended[1:extent_x + 1, 1:extent_y + 1, :]
    beside = extended[2:extent_x + 2, 1:extent_y + 1, :] + extended[0:extent_x, 1:extent_y + 1, :]
    beside = beside + extended[1:extent_x + 1, 2:extent_y + 2, :] + extended[1:extent_x + 1, 0:extent_y, :]
    beside = beside + padded[1:extent_x + 1, 1:extent_y + 1, 2:] + padded[1:extent_x + 1, 1:extent_y + 1, :-2]
    return (6.0 + damping) * centre - beside


def twenty_seven(extended, coefficients):
    extent_x, extent_y, extent_z = coefficients.shape[1], coefficients.shape[2], coefficients.shape[3]
    padded = pad_along(extended, 2)
    summed = jnp.zeros(coefficients.shape[1:], jnp.float32)
    for number, (shift_x, shift_y, shift_z) in enumerate(OFFSETS):
        window = padded[1 + shift_x:1 + shift_x + extent_x, 1 + shift_y:1 + shift_y + extent_y, 1 + shift_z:1 + shift_z + extent_z]
        summed = summed + coefficients[number] * window
    return summed


def restrict_along(extended, along_dim):
    coarse_count = (extended.shape[along_dim] - 2) // 2
    lower_far = lax.slice_in_dim(extended, 0, 2 * coarse_count, 2, along_dim)
    lower_near = lax.slice_in_dim(extended, 1, 2 * coarse_count + 1, 2, along_dim)
    upper_near = lax.slice_in_dim(extended, 2, 2 * coarse_count + 2, 2, along_dim)
    upper_far = lax.slice_in_dim(extended, 3, 2 * coarse_count + 2, 2, along_dim)
    return 0.25 * (lower_far + upper_far) + 0.75 * (lower_near + upper_near)


def prolong_along(extended, along_dim):
    coarse_count = extended.shape[along_dim] - 2
    centre = lax.slice_in_dim(extended, 1, coarse_count + 1, 1, along_dim)
    lower_side = lax.slice_in_dim(extended, 0, coarse_count, 1, along_dim)
    upper_side = lax.slice_in_dim(extended, 2, coarse_count + 2, 1, along_dim)
    even_cells = 0.75 * centre + 0.25 * lower_side
    odd_cells = 0.75 * centre + 0.25 * upper_side
    stacked = jnp.stack([even_cells, odd_cells], axis=along_dim + 1)
    target_shape = list(centre.shape)
    target_shape[along_dim] = 2 * coarse_count
    return stacked.reshape(target_shape)


def restrict_cells(extended):
    reduced = restrict_along(extended, 0)
    reduced = restrict_along(reduced, 1)
    return restrict_along(pad_along(reduced, 2), 2)


def prolong_cells(extended):
    grown = prolong_along(extended, 0)
    grown = prolong_along(grown, 1)
    return prolong_along(pad_along(grown, 2), 2)


def coarse_sweeps(source, coefficients, iterate, count):
    diagonal = coefficients[13]
    for repeat in range(count):
        iterate = iterate + RELAXATION * (source - twenty_seven(pad_plane(iterate), coefficients)) / diagonal
    return iterate


def coarse_cycle(source, operators):
    coefficients = operators[0]
    iterate = RELAXATION * source / coefficients[13]
    if len(operators) == 1:
        return coarse_sweeps(source, coefficients, iterate, CSWEEPS - 1)
    iterate = coarse_sweeps(source, coefficients, iterate, NU - 1)
    residual = source - twenty_seven(pad_plane(iterate), coefficients)
    correction = coarse_cycle(restrict_cells(pad_plane(residual)), operators[1:])
    iterate = iterate + prolong_cells(pad_plane(correction))
    return coarse_sweeps(source, coefficients, iterate, NU)


def fine_sweeps(source, damping, iterate, count):
    for repeat in range(count):
        iterate = iterate + RELAXATION * (source - seven_point(pad_plane(iterate), damping)) / (6.0 + damping)
    return iterate


def reference(source, damping, coarse_one, coarse_two, coarse_three):
    iterate = RELAXATION * source / (6.0 + damping)
    iterate = fine_sweeps(source, damping, iterate, NU - 1)
    residual = source - seven_point(pad_plane(iterate), damping)
    correction = coarse_cycle(restrict_cells(pad_plane(residual)), (coarse_one, coarse_two, coarse_three))
    iterate = iterate + prolong_cells(pad_plane(correction))
    return fine_sweeps(source, damping, iterate, NU)
```

```python
import jax
import jax.numpy as jnp
from jax import lax
from jax.sharding import PartitionSpec as P

NU = 4
CSWEEPS = 8


RELAXATION = 0.8
OFFSETS = tuple(
    (
        (shift_x, shift_y, shift_z)
        for shift_x in (-1, 0, 1)
        for shift_y in (-1, 0, 1)
        for shift_z in (-1, 0, 1)
    )
)


def extended_2(shard, sides, width):
    for axis, dim in sides:
        size, length = (lax.axis_size(axis), shard.shape[dim])
        up = [(i, (i + 1) % size) for i in range(size)]
        down = [(j, i) for i, j in up]
        last = lax.slice_in_dim(shard, length - width, length, axis=dim)
        leading = lax.slice_in_dim(shard, 0, width, axis=dim)
        place = lax.axis_index(axis)
        before = jnp.where(place == 0, 0.0, lax.ppermute(last, axis, up))
        after = jnp.where(place == size - 1, 0.0, lax.ppermute(leading, axis, down))
        shard = jnp.concatenate([before, shard, after], axis=dim)
    return shard


def pad_along(field, along_dim):
    widths = [(0, 0)] * field.ndim
    widths[along_dim] = (1, 1)
    return jnp.pad(field, widths)


def seven_point(extended, damping):
    extent_x, extent_y = (damping.shape[0], damping.shape[1])
    padded = pad_along(extended, 2)
    centre = extended[1 : extent_x + 1, 1 : extent_y + 1, :]
    beside = (
        extended[2 : extent_x + 2, 1 : extent_y + 1, :] + extended[0:extent_x, 1 : extent_y + 1, :]
    )
    beside = (
        beside
        + extended[1 : extent_x + 1, 2 : extent_y + 2, :]
        + extended[1 : extent_x + 1, 0:extent_y, :]
    )
    beside = (
        beside
        + padded[1 : extent_x + 1, 1 : extent_y + 1, 2:]
        + padded[1 : extent_x + 1, 1 : extent_y + 1, :-2]
    )
    return (6.0 + damping) * centre - beside


def twenty_seven(extended, coefficients):
    extent_x, extent_y, extent_z = (
        coefficients.shape[1],
        coefficients.shape[2],
        coefficients.shape[3],
    )
    padded = pad_along(extended, 2)
    summed = jnp.zeros(coefficients.shape[1:], jnp.float32)
    for number, (shift_x, shift_y, shift_z) in enumerate(OFFSETS):
        window = padded[
            1 + shift_x : 1 + shift_x + extent_x,
            1 + shift_y : 1 + shift_y + extent_y,
            1 + shift_z : 1 + shift_z + extent_z,
        ]
        summed = summed + coefficients[number] * window
    return summed


def restrict_along(extended, along_dim):
    coarse_count = (extended.shape[along_dim] - 2) // 2
    lower_far = lax.slice_in_dim(extended, 0, 2 * coarse_count, 2, along_dim)
    lower_near = lax.slice_in_dim(extended, 1, 2 * coarse_count + 1, 2, along_dim)
    upper_near = lax.slice_in_dim(extended, 2, 2 * coarse_count + 2, 2, along_dim)
    upper_far = lax.slice_in_dim(extended, 3, 2 * coarse_count + 2, 2, along_dim)
    return 0.25 * (lower_far + upper_far) + 0.75 * (lower_near + upper_near)


def prolong_along(extended, along_dim):
    coarse_count = extended.shape[along_dim] - 2
    centre = lax.slice_in_dim(extended, 1, coarse_count + 1, 1, along_dim)
    lower_side = lax.slice_in_dim(extended, 0, coarse_count, 1, along_dim)
    upper_side = lax.slice_in_dim(extended, 2, coarse_count + 2, 1, along_dim)
    even_cells = 0.75 * centre + 0.25 * lower_side
    odd_cells = 0.75 * centre + 0.25 * upper_side
    stacked = jnp.stack([even_cells, odd_cells], axis=along_dim + 1)
    target_shape = list(centre.shape)
    target_shape[along_dim] = 2 * coarse_count
    return stacked.reshape(target_shape)


def restrict_cells(extended):
    reduced = restrict_along(extended, 0)
    reduced = restrict_along(reduced, 1)
    return restrict_along(pad_along(reduced, 2), 2)


def prolong_cells(extended):
    grown = prolong_along(extended, 0)
    grown = prolong_along(grown, 1)
    return prolong_along(pad_along(grown, 2), 2)


def rims(field):
    return extended_2(field, (("gx", 0), ("gy", 1)), 1)


def faces(field):
    return extended_2(field, (("gx", 0), ("gy", 1)), 1)


def coarse_sweeps(source, coefficients, iterate, count):
    diagonal = coefficients[13]
    for repeat in range(count):
        iterate = (
            iterate + RELAXATION * (source - twenty_seven(rims(iterate), coefficients)) / diagonal
        )
    return iterate


def coarsest_level(source, coefficients):
    iterate = RELAXATION * source / coefficients[13]
    return coarse_sweeps(source, coefficients, iterate, CSWEEPS - 1)


def coarse_cycle(source, operators):
    coefficients = operators[0]
    if len(operators) == 1:
        return coarsest_level(source, coefficients)
    iterate = RELAXATION * source / coefficients[13]
    iterate = coarse_sweeps(source, coefficients, iterate, NU - 1)
    residual = source - twenty_seven(rims(iterate), coefficients)
    correction = coarse_cycle(restrict_cells(rims(residual)), operators[1:])
    iterate = iterate + prolong_cells(rims(correction))
    return coarse_sweeps(source, coefficients, iterate, NU)


def fine_sweeps(source, damping, iterate, count):
    for repeat in range(count):
        iterate = iterate + RELAXATION * (source - seven_point(faces(iterate), damping)) / (
            6.0 + damping
        )
    return iterate


def on_device(source, damping, coarse_one, coarse_two, coarse_three):
    iterate = RELAXATION * source / (6.0 + damping)
    iterate = fine_sweeps(source, damping, iterate, NU - 1)
    residual = source - seven_point(faces(iterate), damping)
    coarse_source = restrict_cells(rims(residual))
    correction = coarse_cycle(coarse_source, (coarse_one, coarse_two, coarse_three))
    iterate = iterate + prolong_cells(rims(correction))
    return fine_sweeps(source, damping, iterate, NU)


def solution(mesh):
    in_specs = (
        P("gx", "gy", None),
        P("gx", "gy", None),
        P(None, "gx", "gy", None),
        P(None, "gx", "gy", None),
        P(None, "gx", "gy", None),
    )
    out_specs = P("gx", "gy", None)
    return jax.shard_map(
        on_device, mesh=mesh, in_specs=in_specs, out_specs=out_specs, check_vma=False
    )
```

```python
import jax
import jax.numpy as jnp
from jax import lax
from jax.experimental import pallas as pl
from jax.experimental.pallas import tpu as pltpu
from jax.sharding import PartitionSpec as P

F32 = jnp.float32
RELAXATION = 0.8
KEEP = 1.0 - RELAXATION
N = 16
HI = lax.Precision.HIGHEST


def ring(value, axis, step):
    return lax.ppermute(value, axis, [(i, (i + step) % N) for i in range(N)])


def everyone(block, axis):
    copies = jnp.broadcast_to(block[None], (N,) + block.shape)
    return lax.all_to_all(copies, axis, 0, 0)


def iota(shape, dim):
    return lax.broadcasted_iota(jnp.int32, shape, dim)


def weight(fine, coarse):
    d = fine - 2 * coarse
    return jnp.where((d == 0) | (d == 1), 0.75, jnp.where((d == -1) | (d == 2), 0.25, 0.0))


def matrix(rows, lanes, entry):
    return entry(iota((rows, lanes), 0), iota((rows, lanes), 1)).astype(F32)


def dot(a, b):
    return jnp.dot(a, b, precision=HI, preferred_element_type=F32)


def batch(lo, hi, group, compute, store):
    def some(indices):
        for i, value in [(i, compute(i)) for i in indices]:
            store(i, value)

    count = (hi - lo) // group
    if count == 1:
        some(range(lo, lo + group))
    elif count > 1:
        lax.fori_loop(
            0, count, lambda n, c: (some([lo + n * group + i for i in range(group)]), c)[1], 0
        )
    if lo + count * group < hi:
        some(range(lo + count * group, hi))


def put(ref):
    def store(i, value):
        ref[i] = value

    return store


def rows_valid(shape, first, count):
    row = iota(shape, 0) + first
    return (row >= 0) & (row < count)


def between(i, count):
    return (i >= 0) & (i < count)


def z_shifts(c, period):
    lane = iota(c.shape, 1) & (period - 1)
    size = c.shape[1]
    below = jnp.where(lane > 0, pltpu.roll(c, 1, 1), 0.0)
    above = jnp.where(lane < period - 1, pltpu.roll(c, size - 1, 1), 0.0)
    return below, above


def grow_rows(coarse, ref, index, count):
    mid = 0.75 * coarse[4 : 4 + count]
    ref[index, pl.ds(0, count, stride=2), :] = mid + 0.25 * coarse[3 : 3 + count]
    ref[index, pl.ds(1, count, stride=2), :] = mid + 0.25 * coarse[5 : 5 + count]


def halve_rows(ref, index, count):
    part = [ref[index, pl.ds(7 + i, count, stride=2), :] for i in range(4)]
    return 0.25 * (part[0] + part[3]) + 0.75 * (part[1] + part[2])


def six(before, c, after):
    rows = c.shape[0]
    below, above = z_shifts(c, c.shape[1])
    return before + after + pltpu.roll(c, 1, 0) + pltpu.roll(c, rows - 1, 0) + below + above


def fine_down(
    pos, source, damping, xlo, xhi, ylo, yhi, v_out, g_out, s_out, w_out, a, b, s, w, t
):
    ix, iy = pos[0], pos[1]
    row_ok = rows_valid((48, 256), iy * 32 - 8, 512)

    def start(lo, hi, s_mid, d_mid):
        def compute(p):
            ok = row_ok & between(ix * 8 + p - 7, 128)
            rows = jnp.concatenate([ylo[0, p], s_mid(p - lo), yhi[0, p]], axis=0)
            damp = jnp.concatenate([ylo[1, p], d_mid(p - lo), yhi[1, p]], axis=0)
            return rows, jnp.where(ok, RELAXATION / (6.0 + damp), 0.0)

        def store(p, value):
            s[p], w[p] = value
            a[p] = value[0] * value[1]

        batch(lo, hi, 1, compute, store)

    start(0, 7, lambda i: xlo[0, i], lambda i: xlo[1, i])
    start(7, 15, lambda i: source[i], lambda i: damping[i])
    start(15, 22, lambda i: xhi[0, i], lambda i: xhi[1, i])

    def sweep(src, dst, lo, hi, off):
        def compute(p):
            c = src[p]
            return KEEP * c + w[p] * (s[p] + six(src[p - 1], c, src[p + 1]))

        def store(p, value):
            dst[p - off] = value

        batch(lo, hi, 2, compute, store)

    sweep(a, b, 1, 21, 0)
    sweep(b, a, 2, 20, 0)
    sweep(a, v_out, 3, 19, 3)

    def residual(mid, first):
        def compute(p):
            ok = row_ok & between(ix * 8 + p - 7, 128)
            damp = jnp.concatenate([ylo[1, p], mid(p - first), yhi[1, p]], axis=0)
            c = v_out[p - 3]
            r = s[p] + six(v_out[p - 4], c, v_out[p - 2]) - (6.0 + damp) * c
            return jnp.where(ok, r, 0.0)

        return compute

    batch(4, 7, 3, residual(lambda i: xlo[1, i], 0), put(b))
    batch(7, 15, 2, residual(lambda i: damping[i], 7), put(b))
    batch(15, 18, 3, residual(lambda i: xhi[1, i], 15), put(b))
    s_out[...] = s[3:19]
    w_out[...] = w[3:19]

    rz = matrix(256, 128, weight)

    def coarse(j):
        q = 2 * j + 4
        return dot(0.25 * (b[q] + b[q + 3]) + 0.75 * (b[q + 1] + b[q + 2]), rz)

    batch(0, 6, 6, coarse, put(t))
    batch(0, 6, 6, lambda j: halve_rows(t, j, 16), put(g_out))


def fine_up(pos, s, w, v_in, c1, out, a, b, u):
    ix, iy = pos[0], pos[1]
    row_ok = rows_valid((48, 256), iy * 32 - 8, 512)
    coarse_ok = rows_valid((32, 128), iy * 16 - 8, 256)
    for q in range(10):
        ok = coarse_ok & between(ix * 4 + q - 3, 64)
        grow_rows(jnp.where(ok, c1[q], 0.0), u, q, 24)

    pz = matrix(128, 256, lambda j, f: weight(f, j))

    def add(f):
        ok = row_ok & between(ix * 8 + f - 4, 128)
        h = f // 2
        fine = dot(0.75 * u[h + 1] + 0.25 * u[h + 2 * (f % 2)], pz)
        return v_in[f] + jnp.where(ok, fine, 0.0)

    for h in range(0, 16, 4):
        batch(h, h + 4, 4, add, put(a))

    def sweep(src, dst, lo, hi, keep_rows):
        def compute(p):
            c = src[p]
            return KEEP * c + w[p] * (s[p] + six(src[p - 1], c, src[p + 1]))

        def store(p, value):
            if keep_rows:
                dst[p - lo] = value[8:40]
            else:
                dst[p] = value

        batch(lo, hi, 2, compute, store)

    sweep(a, b, 1, 15, False)
    sweep(b, a, 2, 14, False)
    sweep(a, b, 3, 13, False)
    sweep(b, out, 4, 12, True)


def one_coefficient(cx, clo, chi, k, p):
    return jnp.concatenate([clo[k, p], cx[k, p], chi[k, p]], axis=0)


def one_weights(w, cx, clo, chi, ix, iy):
    def compute(p):
        ok = rows_valid((32, 128), iy * 16 - 8, 256) & between(ix * 4 + p - 4, 64)
        return jnp.where(ok, RELAXATION / one_coefficient(cx, clo, chi, 13, p), 0.0)

    batch(0, 12, 4, compute, put(w))


def one_spread(v, vz, lo, hi):
    def compute(p):
        c = v[p]
        below, above = z_shifts(c, 128)
        return below, c, above

    def store(p, value):
        for i in range(3):
            vz[i, p] = value[i]

    batch(lo, hi, 4, compute, store)


def one_others(vz, cx, clo, chi, p, cp):
    parts = []
    for a in range(3):
        total = None
        for c in range(3):
            plane = vz[c, p + a - 1]
            for b in range(3):
                k = 9 * a + 3 * b + c
                if k == 13:
                    continue
                moved = plane if b == 1 else pltpu.roll(plane, 1 if b == 0 else 31, 0)
                term = one_coefficient(cx, clo, chi, k, cp) * moved
                total = term if total is None else total + term
        parts.append(total)
    return parts[0] + parts[1] + parts[2]


def one_down(pos, g, cx, clo, chi, g_out, v_out, v, vz, w, t):
    ix, iy = pos[0], pos[1]
    one_weights(w, cx, clo, chi, ix, iy)
    row_ok = rows_valid((32, 128), iy * 16 - 8, 256)
    for p in (0, 13):
        v[p] = jnp.where(row_ok & between(ix * 4 + p - 5, 64), g[p], 0.0)
    batch(1, 13, 4, lambda p: w[p - 1] * g[p], put(v))

    def update(p):
        rest = one_others(vz, cx, clo, chi, p, p - 1)
        return KEEP * v[p] + w[p - 1] * (g[p] - rest)

    for k in range(3):
        one_spread(v, vz, k, 14 - k)
        batch(1 + k, 13 - k, 2, update, put(v))
    one_spread(v, vz, 3, 11)

    def residual(p):
        ok = row_ok & between(ix * 4 + p - 5, 64)
        rest = one_others(vz, cx, clo, chi, p, p - 1)
        own = one_coefficient(cx, clo, chi, 13, p - 1) * vz[1, p]
        return jnp.where(ok, g[p] - own - rest, 0.0)

    batch(4, 10, 2, residual, put(v))
    for p in range(4):
        v_out[p] = vz[1, p + 5, 8:24]
    total = None
    for j in range(2):
        q = 2 * j + 4
        t[j] = 0.25 * (v[q] + v[q + 3]) + 0.75 * (v[q + 1] + v[q + 2])
    for j in range(2):
        rz = matrix(128, 128, lambda f, m: jnp.where(m >> 6 == j, weight(f, m & 63), 0.0))
        term = dot(halve_rows(t, j, 8), rz)
        total = term if total is None else total + term
    g_out[...] = total


def two_coefficient(c2, block, k):
    ref, index = c2[block]
    parts = []
    for j in range(3):
        rows = pl.ds((j * 27 + k) * 8, 8)
        parts.append(ref[rows, :] if index is None else ref[index, rows, :])
    return jnp.concatenate(parts, axis=0)


def two_blocks(far_lo, before, own, after, far_hi):
    return [(far_lo, 0), (far_lo, 1), (before, None), (own, None), (after, None)] + [
        (far_hi, 0),
        (far_hi, 1),
    ]


def two_weights(w, c2, ix, iy):
    row_ok = rows_valid((24, 128), iy * 8 - 8, 128)

    def compute(b):
        ok = row_ok & between(ix + b - 3, 16)
        return jnp.where(ok, RELAXATION / two_coefficient(c2, b, 13), 0.0)

    batch(0, 7, 7, compute, put(w))


def two_spread(v, vx, lo, hi):
    low = iota((24, 128), 1) < 64
    turned = {b: pltpu.roll(v[b], 64, 1) for b in range(lo - 1, hi + 1)}
    for b in range(lo, hi):
        moved = (
            jnp.where(low, turned[b - 1], turned[b]),
            v[b],
            jnp.where(low, turned[b], turned[b + 1]),
        )
        for a, c in enumerate(moved):
            vx[3 * a, b], vx[3 * a + 2, b] = z_shifts(c, 64)
            vx[3 * a + 1, b] = c


def two_others(vx, c2, b):
    parts = []
    for a in range(3):
        total = None
        for c in range(3):
            plane = vx[3 * a + c, b]
            for s in range(3):
                k = 9 * a + 3 * s + c
                if k == 13:
                    continue
                moved = plane if s == 1 else pltpu.roll(plane, 1 if s == 0 else 23, 0)
                term = two_coefficient(c2, b - 1, k) * moved
                total = term if total is None else total + term
        parts.append(total)
    return parts[0] + parts[1] + parts[2]


def two_sweep(v, vx, w, g, c2, lo, hi):
    two_spread(v, vx, lo, hi)

    def compute(b):
        return KEEP * v[b] + w[b - 1] * (g[b - 1] - two_others(vx, c2, b))

    batch(lo, hi, hi - lo, compute, put(v))


def twice(step):
    lax.fori_loop(0, 2, lambda _, c: (step(), c)[1], 0)


def two_sources(g, own, ix):
    batch(0, 7, 7, lambda b: g[jnp.clip(ix + b - 3, 0, 15)], put(own))


def two_down(
    pos, g_all, far_lo, before, own, after, far_hi, g_out, v_out, v, vx, w, g, t
):
    ix, iy = pos[0], pos[1]
    c2 = two_blocks(far_lo, before, own, after, far_hi)
    two_weights(w, c2, ix, iy)
    two_sources(g_all, g, ix)
    for b in (0, 8):
        v[b] = jnp.zeros((24, 128), F32)
    batch(1, 8, 7, lambda b: w[b - 1] * g[b - 1], put(v))
    twice(lambda: two_sweep(v, vx, w, g, c2, 2, 7))
    two_sweep(v, vx, w, g, c2, 3, 6)
    two_spread(v, vx, 3, 6)
    v_out[...] = v[4, 8:16]
    row_ok = rows_valid((24, 128), iy * 8 - 8, 128)

    def residual(b):
        rest = two_coefficient(c2, b - 1, 13) * v[b] + two_others(vx, c2, b)
        return jnp.where(row_ok & between(ix + b - 4, 16), g[b - 1] - rest, 0.0)

    batch(3, 6, 3, residual, put(v))
    low = iota((24, 128), 1) < 64
    here = 0.75 * v[4] + 0.25 * jnp.where(low, v[5], v[3])
    t[0] = dot(here, matrix(128, 128, lambda f, m: weight(f & 63, m & 31)))
    y = halve_rows(t, 0, 4)
    y = jnp.where(iota((4, 128), 1) >> 5 == iota((4, 128), 0), y, 0.0)
    g_out[...] = jnp.broadcast_to(jnp.sum(y, axis=0, keepdims=True), (8, 128))


def three_y(c):
    lane = iota(c.shape, 1)
    rows = c.shape[0]
    down = pltpu.roll(c, 32, 1)
    below = jnp.where(lane >= 32, down, pltpu.roll(down, 1, 0))
    up = pltpu.roll(c, 96, 1)
    above = jnp.where(lane < 96, up, pltpu.roll(up, rows - 1, 0))
    return below, above


def three_solve(v, vx, w, g, c3, iy):
    yb = iota((8, 128), 0)
    ok = (yb + iy >= 3) & (yb + iy < 19) & (yb < 7)

    def coefficient(x, k):
        return c3[x, pl.ds(k * 8, 8), :]

    for x in (0, 17):
        v[x] = jnp.zeros((8, 128), F32)
        for k in range(9):
            vx[k, x] = jnp.zeros((8, 128), F32)
    batch(
        0, 16, 16, lambda x: jnp.where(ok, RELAXATION / coefficient(x, 13), 0.0), put(w)
    )
    for x in range(16):
        v[x + 1] = w[x] * g[x, 0:8]

    def spread(x):
        c = v[x]
        below, above = three_y(c)
        values = []
        for plane in (below, c, above):
            left, right = z_shifts(plane, 32)
            values += [left, plane, right]
        return values

    def keep(x, values):
        for k in range(9):
            vx[k, x] = values[k]

    def update(x):
        parts = []
        for a in range(3):
            part = None
            for m in range(9):
                k = 9 * a + m
                if k == 13:
                    continue
                term = coefficient(x - 1, k) * vx[m, x + a - 1]
                part = term if part is None else part + term
            parts.append(part)
        rest = parts[0] + parts[1] + parts[2]
        return KEEP * v[x] + w[x - 1] * (g[x - 1, 0:8] - rest)

    def sweep(_, carry):
        for x in (1, 5, 9, 13):
            batch(x, x + 4, 4, spread, keep)
        for x in (1, 5, 9, 13):
            batch(x, x + 4, 4, update, put(v))
        return carry

    lax.fori_loop(0, 7, sweep, 0)


def coarse_up(
    pos, gv, c3, g2_all, far_lo, before, own, after, far_hi, g1, v1, v1lo, v1hi,
    cx, clo, chi, out,
    s3, vx3, w3, e, d, pc, s2, vx2, w2, g2, u, s1, vz, w1,
):
    ix, iy = pos[0], pos[1]
    c2 = two_blocks(far_lo, before, own, after, far_hi)
    three_solve(s3, vx3, w3, gv, c3, iy)
    two_weights(w2, c2, ix, iy)
    two_sources(g2_all, g2, ix)
    one_weights(w1, cx, clo, chi, ix, iy)
    for j in range(9):
        x = jnp.clip(ix + j - 4, 0, 15)
        mid = 0.75 * s3[x + 1]
        for p in range(2):
            c = mid + 0.25 * s3[x + 2 * p]
            below, above = three_y(c)
            e[0, j, :, p * 128 : p * 128 + 128] = 0.75 * c + 0.25 * below
            e[1, j, :, p * 128 : p * 128 + 128] = 0.75 * c + 0.25 * above
    for q in range(4):

        def entry(r, m):
            same = (r >> 7 == m >> 6) & ((r >> 5) & 3 == q)
            return jnp.where(same, weight(m & 63, r & 31), 0.0)

        pz2 = matrix(256, 128, entry)
        for s in range(2):
            d[4 * s + q] = dot(e[s].reshape(72, 256), pz2).reshape(9, 8, 128)
    for s in range(2):
        for q in range(4):
            for j in range(9):
                pc[j, pl.ds(2 * q + s, 8, stride=8), :] = d[4 * s + q, j]
    row_two = rows_valid((24, 128), iy * 8 - 8, 128)
    for j in range(9):
        ok = row_two & between(ix + j - 4, 16)
        held = gv[jnp.clip(ix + j - 4, 0, 15), 8:32]
        s2[j] = jnp.where(ok, held + pc[j, 16:40], 0.0)
    for lo, hi in ((1, 8), (2, 7)):
        twice(lambda: two_sweep(s2, vx2, w2, g2, c2, lo, hi))
    low = iota((24, 128), 1) < 64
    for k in range(3):
        lo, here, hi = s2[k + 2], s2[k + 3], s2[k + 4]
        grow_rows(jnp.where(low, 0.75 * here, 0.25 * lo), u, 4 * k, 16)
        grow_rows(jnp.where(low, 0.75, 0.25) * here, u, 4 * k + 1, 16)
        grow_rows(jnp.where(low, 0.25, 0.75) * here, u, 4 * k + 2, 16)
        grow_rows(jnp.where(low, 0.25 * hi, 0.75 * here), u, 4 * k + 3, 16)
    row_one = rows_valid((32, 128), iy * 16 - 8, 256)
    pz1 = matrix(128, 128, lambda r, f: weight(f, r & 63))

    def add(p):
        ok = row_one & between(ix * 4 + p - 4, 64)
        held = jnp.concatenate([v1lo[p], v1[p], v1hi[p]], axis=0)
        return jnp.where(ok, held + dot(u[p], pz1), 0.0)

    for p in (0, 4, 8):
        batch(p, p + 4, 4, add, put(s1))

    def update(p):
        rest = one_others(vz, cx, clo, chi, p, p)
        return KEEP * s1[p] + w1[p] * (g1[p + 1] - rest)

    for k in range(4):
        one_spread(s1, vz, k, 12 - k)
        batch(1 + k, 11 - k, 2, update, put(s1))
    for p in range(4):
        out[p] = s1[p + 4, 8:24]


def vm(*shape):
    return pltpu.VMEM(shape, F32)


def call(kernel, name, outs, scratch, pos, *operands):
    shapes = [jax.ShapeDtypeStruct(s, F32) for s in outs]
    return pl.pallas_call(
        kernel,
        name=name,
        out_shape=shapes,
        in_specs=[pl.BlockSpec(memory_space=pltpu.SMEM)]
        + [pl.BlockSpec(memory_space=pltpu.VMEM)] * len(operands),
        out_specs=[pl.BlockSpec(memory_space=pltpu.VMEM)] * len(outs),
        scratch_shapes=scratch,
        compiler_params=pltpu.CompilerParams(vmem_limit_bytes=50 * 2**20),
    )(pos, *operands)


def both(value, axis, dim, width):
    length = value.shape[dim]
    last = lax.slice_in_dim(value, length - width, length, axis=dim)
    first = lax.slice_in_dim(value, 0, width, axis=dim)
    return ring(last, axis, 1), ring(first, axis, -1)


def wide(value, axis, dim, width):
    before, after = both(value, axis, dim, width)
    return jnp.concatenate([before, value, after], axis=dim)


def after_all(value, *others):
    return lax.optimization_barrier((value,) + others)[0]


def on_device(source, damping, coarse_one, coarse_two, coarse_three):
    pos = jnp.stack([lax.axis_index("gx"), lax.axis_index("gy")]).astype(jnp.int32)

    with jax.named_scope("fine_halo"):
        last = jnp.stack([source[1:], damping[1:]])
        first = jnp.stack([source[:7], damping[:7]])
        xlo, xhi = ring(last, "gx", 1), ring(first, "gx", -1)

    with jax.named_scope("two_three_halo"):
        coarse_two, coarse_three, one = lax.optimization_barrier(
            (coarse_two, coarse_three, coarse_one, last, first)
        )[:3]
        c2 = jnp.concatenate([coarse_two[:, 0], coarse_two[:, 1]], axis=-1)
        c3 = jnp.concatenate([coarse_three[:, 0, i] for i in range(4)], axis=-1)
        c3 = jnp.pad(c3, ((0, 5), (0, 0)))
        own = jnp.concatenate([c2.reshape(216, 128), c3], axis=0)
        before, after = ring(own, "gy", 1), ring(own, "gy", -1)
        two = jnp.concatenate([before[:216], own[:216], after[:216]])
        three = jnp.stack([before[216:], c3, after[216:]])
        far_before, far_after = ring(three, "gy", 2), ring(three, "gy", -2)
        seven = jnp.concatenate([far_before[:2], three, far_after[1:], c3[None]])
        seven = jnp.transpose(seven[:, :27], (1, 0, 2)).reshape(216, 128)
        c3 = lax.all_gather(seven, "gx")
        one_lo, one_hi = both(one, "gy", 2, 8)

    with jax.named_scope("fine_halo"):
        edge = []
        for rows in (slice(24, 32), slice(0, 8)):
            mid = jnp.stack([source[:, rows], damping[:, rows]])
            edge.append(jnp.concatenate([xlo[:, :, rows], mid, xhi[:, :, rows]], axis=1))
        ylo, yhi = ring(edge[0], "gy", 1), ring(edge[1], "gy", -1)

    with jax.named_scope("one_halo"):
        cxlo, cxhi = both(after_all(coarse_one, *edge), "gx", 1, 4)

    with jax.named_scope("fine_down"):
        v0, g1, s0, w0 = call(
            fine_down, "fine_down",
            [(16, 48, 256), (6, 16, 128), (16, 48, 256), (16, 48, 256)],
            [vm(22, 48, 256)] * 4 + [vm(6, 48, 128)],
            pos, source, damping, xlo, xhi, ylo, yhi,
        )

    with jax.named_scope("one_halo"):
        cxlo, cxhi, g1 = lax.optimization_barrier((cxlo, cxhi, g1))
        sides = jnp.concatenate([cxlo, cxhi], axis=1)
        side_lo, side_hi = both(sides, "gy", 2, 8)
        cx = jnp.concatenate([cxlo, coarse_one, cxhi], axis=1)

    with jax.named_scope("one_exchange"):
        edge_lo = RELAXATION * g1[0:1] / cxlo[13, 3:4]
        edge_hi = RELAXATION * g1[5:6] / cxhi[13, 0:1]
        up = jnp.concatenate([edge_lo, g1[1:5]])
        down = jnp.concatenate([g1[1:5], edge_hi])
        before, after = ring(up, "gx", 1), ring(down, "gx", -1)
        g1e = wide(jnp.concatenate([before, g1[1:5], after]), "gy", 1, 8)

    with jax.named_scope("two_halo"):
        two = after_all(two, up, down)
        tlo, thi = ring(two, "gx", 1), ring(two, "gx", -1)
        above, below = jnp.stack([two, thi]), jnp.stack([tlo, two])
        far_lo, far_hi = ring(above, "gx", 3), ring(below, "gx", -3)
        blocks = (far_lo, tlo, two, thi, far_hi)

    with jax.named_scope("one_down"):
        g1e = after_all(g1e, above, below)
        clo = jnp.concatenate([side_lo[:, :4], one_lo, side_lo[:, 4:]], axis=1)
        chi = jnp.concatenate([side_hi[:, :4], one_hi, side_hi[:, 4:]], axis=1)
        g2, v1 = call(
            one_down, "one_down", [(8, 128), (4, 16, 128)],
            [vm(14, 32, 128), vm(3, 14, 32, 128), vm(12, 32, 128), vm(2, 32, 128)],
            pos, g1e, cx, clo, chi,
        )

    with jax.named_scope("two_exchange"):
        g2e = everyone(wide(g2, "gy", 0, 8), "gx")

    with jax.named_scope("one_values"):
        v1 = wide(v1, "gx", 0, 4)

    with jax.named_scope("two_down"):
        g3, v2 = call(
            two_down, "two_down", [(8, 128), (8, 128)],
            [
                vm(9, 24, 128), vm(9, 9, 24, 128), vm(7, 24, 128), vm(7, 24, 128),
                vm(1, 24, 128),
            ],
            pos, g2e, *blocks,
        )

    with jax.named_scope("three_exchange"):
        up = jnp.concatenate([g3, v2, v1[:, 8:].reshape(96, 128)])
        down = jnp.concatenate([g3, v2, v1[:, :8].reshape(96, 128)])
        before, after = ring(up, "gy", 1), ring(down, "gy", -1)
        v1lo, v1hi = before[16:].reshape(12, 8, 128), after[16:].reshape(12, 8, 128)
        trip = jnp.concatenate([before[:1], g3[:1], after[:1]])
        far_before, far_after = ring(trip, "gy", 2), ring(trip, "gy", -2)
        gv = everyone(
            jnp.concatenate(
                [far_before[:2], trip, far_after[1:], g3[:1], before[8:16], v2, after[8:16]]
            ),
            "gx",
        )

    with jax.named_scope("coarse_up"):
        (c1,) = call(
            coarse_up, "coarse_up", [(4, 16, 128)],
            [
                vm(18, 8, 128), vm(9, 18, 8, 128), vm(16, 8, 128), vm(2, 9, 8, 256),
                vm(8, 9, 8, 128), vm(9, 64, 128),
                vm(9, 24, 128), vm(9, 9, 24, 128), vm(7, 24, 128), vm(7, 24, 128),
                vm(12, 32, 128), vm(12, 32, 128), vm(3, 12, 32, 128), vm(12, 32, 128),
            ],
            pos, gv, c3, g2e, *blocks, g1e, v1, v1lo, v1hi, cx, clo, chi,
        )

    with jax.named_scope("one_back"):
        c1e = wide(wide(c1, "gx", 0, 3), "gy", 1, 8)

    with jax.named_scope("fine_up"):
        (out,) = call(
            fine_up, "fine_up", [(8, 32, 256)],
            [vm(16, 48, 256)] * 2 + [vm(10, 48, 128)], pos, s0, w0, v0, c1e,
        )
    return out


def solution(mesh):
    in_specs = (
        P("gx", "gy", None),
        P("gx", "gy", None),
        P(None, "gx", "gy", None),
        P(None, "gx", "gy", None),
        P(None, "gx", "gy", None),
    )
    return jax.shard_map(
        on_device, mesh=mesh, in_specs=in_specs, out_specs=P("gx", "gy", None), check_vma=False
    )
```

```python
import jax
import jax.numpy as jnp
from jax import lax
from jax.experimental import pallas as pl
from jax.experimental.pallas import tpu as pltpu
from jax.sharding import PartitionSpec as P

F32 = jnp.float32
RELAXATION = 0.8
KEEP = 1.0 - RELAXATION
N = 16
HI = lax.Precision.HIGHEST


def ring(value, axis, step):
    return lax.ppermute(value, axis, [(i, (i + step) % N) for i in range(N)])


def everyone(block, axis):
    copies = jnp.broadcast_to(block[None], (N,) + block.shape)
    return lax.all_to_all(copies, axis, 0, 0)


def iota(shape, dim):
    return lax.broadcasted_iota(jnp.int32, shape, dim)


def weight(fine, coarse):
    d = fine - 2 * coarse
    return jnp.where((d == 0) | (d == 1), 0.75, jnp.where((d == -1) | (d == 2), 0.25, 0.0))


def matrix(rows, lanes, entry):
    return entry(iota((rows, lanes), 0), iota((rows, lanes), 1)).astype(F32)


def dot(a, b):
    return jnp.dot(a, b, precision=HI, preferred_element_type=F32)


def batch(lo, hi, group, compute, store):
    def some(indices):
        for i, value in [(i, compute(i)) for i in indices]:
            store(i, value)

    count = (hi - lo) // group
    if count == 1:
        some(range(lo, lo + group))
    elif count > 1:
        lax.fori_loop(
            0, count, lambda n, c: (some([lo + n * group + i for i in range(group)]), c)[1], 0
        )
    if lo + count * group < hi:
        some(range(lo + count * group, hi))


def put(ref):
    def store(i, value):
        ref[i] = value

    return store


def rows_valid(shape, first, count):
    row = iota(shape, 0) + first
    return (row >= 0) & (row < count)


def between(i, count):
    return (i >= 0) & (i < count)


def z_shifts(c, period):
    lane = iota(c.shape, 1) & (period - 1)
    size = c.shape[1]
    below = jnp.where(lane > 0, pltpu.roll(c, 1, 1), 0.0)
    above = jnp.where(lane < period - 1, pltpu.roll(c, size - 1, 1), 0.0)
    return below, above


def grow_rows(coarse, ref, index, count):
    mid = 0.75 * coarse[4 : 4 + count]
    ref[index, pl.ds(0, count, stride=2), :] = mid + 0.25 * coarse[3 : 3 + count]
    ref[index, pl.ds(1, count, stride=2), :] = mid + 0.25 * coarse[5 : 5 + count]


def halve_rows(ref, index, count):
    part = [ref[index, pl.ds(7 + i, count, stride=2), :] for i in range(4)]
    return 0.25 * (part[0] + part[3]) + 0.75 * (part[1] + part[2])


def six(before, c, after):
    rows = c.shape[0]
    below, above = z_shifts(c, c.shape[1])
    return before + after + pltpu.roll(c, 1, 0) + pltpu.roll(c, rows - 1, 0) + below + above


def fine_down(
    pos, source, damping, xlo, xhi, ylo, yhi, v_out, g_out, s_out, w_out, a, b, s, w, t
):
    ix, iy = pos[0], pos[1]
    row_ok = rows_valid((48, 256), iy * 32 - 8, 512)

    def start(lo, hi, s_mid, d_mid):
        def compute(p):
            ok = row_ok & between(ix * 8 + p - 7, 128)
            rows = jnp.concatenate([ylo[0, p], s_mid(p - lo), yhi[0, p]], axis=0)
            damp = jnp.concatenate([ylo[1, p], d_mid(p - lo), yhi[1, p]], axis=0)
            return rows, jnp.where(ok, RELAXATION / (6.0 + damp), 0.0)

        def store(p, value):
            s[p], w[p] = value
            a[p] = value[0] * value[1]

        batch(lo, hi, 1, compute, store)

    start(0, 7, lambda i: xlo[0, i], lambda i: xlo[1, i])
    start(7, 15, lambda i: source[i], lambda i: damping[i])
    start(15, 22, lambda i: xhi[0, i], lambda i: xhi[1, i])

    def sweep(src, dst, lo, hi, off):
        def compute(p):
            c = src[p]
            return KEEP * c + w[p] * (s[p] + six(src[p - 1], c, src[p + 1]))

        def store(p, value):
            dst[p - off] = value

        batch(lo, hi, 2, compute, store)

    sweep(a, b, 1, 21, 0)
    sweep(b, a, 2, 20, 0)
    sweep(a, v_out, 3, 19, 3)

    def residual(mid, first):
        def compute(p):
            ok = row_ok & between(ix * 8 + p - 7, 128)
            damp = jnp.concatenate([ylo[1, p], mid(p - first), yhi[1, p]], axis=0)
            c = v_out[p - 3]
            r = s[p] + six(v_out[p - 4], c, v_out[p - 2]) - (6.0 + damp) * c
            return jnp.where(ok, r, 0.0)

        return compute

    batch(4, 7, 3, residual(lambda i: xlo[1, i], 0), put(b))
    batch(7, 15, 2, residual(lambda i: damping[i], 7), put(b))
    batch(15, 18, 3, residual(lambda i: xhi[1, i], 15), put(b))
    s_out[...] = s[3:19]
    w_out[...] = w[3:19]

    rz = matrix(256, 128, weight)

    def coarse(j):
        q = 2 * j + 4
        return dot(0.25 * (b[q] + b[q + 3]) + 0.75 * (b[q + 1] + b[q + 2]), rz)

    batch(0, 6, 6, coarse, put(t))
    batch(0, 6, 6, lambda j: halve_rows(t, j, 16), put(g_out))


def fine_up(pos, s, w, v_in, c1, out, a, b, u):
    ix, iy = pos[0], pos[1]
    row_ok = rows_valid((48, 256), iy * 32 - 8, 512)
    coarse_ok = rows_valid((32, 128), iy * 16 - 8, 256)
    for q in range(10):
        ok = coarse_ok & between(ix * 4 + q - 3, 64)
        grow_rows(jnp.where(ok, c1[q], 0.0), u, q, 24)

    pz = matrix(128, 256, lambda j, f: weight(f, j))

    def add(f):
        ok = row_ok & between(ix * 8 + f - 4, 128)
        h = f // 2
        fine = dot(0.75 * u[h + 1] + 0.25 * u[h + 2 * (f % 2)], pz)
        return v_in[f] + jnp.where(ok, fine, 0.0)

    for h in range(0, 16, 4):
        batch(h, h + 4, 4, add, put(a))

    def sweep(src, dst, lo, hi, keep_rows):
        def compute(p):
            c = src[p]
            return KEEP * c + w[p] * (s[p] + six(src[p - 1], c, src[p + 1]))

        def store(p, value):
            if keep_rows:
                dst[p - lo] = value[8:40]
            else:
                dst[p] = value

        batch(lo, hi, 2, compute, store)

    sweep(a, b, 1, 15, False)
    sweep(b, a, 2, 14, False)
    sweep(a, b, 3, 13, False)
    sweep(b, out, 4, 12, True)


def one_coefficient(cx, clo, chi, k, p):
    return jnp.concatenate([clo[k, p], cx[k, p], chi[k, p]], axis=0)


def one_weights(w, cx, clo, chi, ix, iy):
    def compute(p):
        ok = rows_valid((32, 128), iy * 16 - 8, 256) & between(ix * 4 + p - 4, 64)
        return jnp.where(ok, RELAXATION / one_coefficient(cx, clo, chi, 13, p), 0.0)

    batch(0, 12, 4, compute, put(w))


def one_spread(v, vz, lo, hi):
    def compute(p):
        c = v[p]
        below, above = z_shifts(c, 128)
        return below, c, above

    def store(p, value):
        for i in range(3):
            vz[i, p] = value[i]

    batch(lo, hi, 4, compute, store)


def one_others(vz, cx, clo, chi, p, cp):
    parts = []
    for a in range(3):
        total = None
        for c in range(3):
            plane = vz[c, p + a - 1]
            for b in range(3):
                k = 9 * a + 3 * b + c
                if k == 13:
                    continue
                moved = plane if b == 1 else pltpu.roll(plane, 1 if b == 0 else 31, 0)
                term = one_coefficient(cx, clo, chi, k, cp) * moved
                total = term if total is None else total + term
        parts.append(total)
    return parts[0] + parts[1] + parts[2]


def one_down(pos, g, cx, clo, chi, g_out, v_out, v, vz, w, t):
    ix, iy = pos[0], pos[1]
    one_weights(w, cx, clo, chi, ix, iy)
    row_ok = rows_valid((32, 128), iy * 16 - 8, 256)
    for p in (0, 13):
        v[p] = jnp.where(row_ok & between(ix * 4 + p - 5, 64), g[p], 0.0)
    batch(1, 13, 4, lambda p: w[p - 1] * g[p], put(v))

    def update(p):
        rest = one_others(vz, cx, clo, chi, p, p - 1)
        return KEEP * v[p] + w[p - 1] * (g[p] - rest)

    for k in range(3):
        one_spread(v, vz, k, 14 - k)
        batch(1 + k, 13 - k, 2, update, put(v))
    one_spread(v, vz, 3, 11)

    def residual(p):
        ok = row_ok & between(ix * 4 + p - 5, 64)
        rest = one_others(vz, cx, clo, chi, p, p - 1)
        own = one_coefficient(cx, clo, chi, 13, p - 1) * vz[1, p]
        return jnp.where(ok, g[p] - own - rest, 0.0)

    batch(4, 10, 2, residual, put(v))
    for p in range(4):
        v_out[p] = vz[1, p + 5, 8:24]
    total = None
    for j in range(2):
        q = 2 * j + 4
        t[j] = 0.25 * (v[q] + v[q + 3]) + 0.75 * (v[q + 1] + v[q + 2])
    for j in range(2):
        rz = matrix(128, 128, lambda f, m: jnp.where(m >> 6 == j, weight(f, m & 63), 0.0))
        term = dot(halve_rows(t, j, 8), rz)
        total = term if total is None else total + term
    g_out[...] = total


def two_coefficient(c2, block, k):
    return jnp.concatenate([ref[block, pl.ds(k * 8, 8), :] for ref in c2], axis=0)


def two_weights(w, c2, ix, iy):
    row_ok = rows_valid((24, 128), iy * 8 - 8, 128)

    def compute(b):
        ok = row_ok & between(ix + b - 3, 16)
        return jnp.where(ok, RELAXATION / two_coefficient(c2, b, 13), 0.0)

    batch(0, 7, 7, compute, put(w))


def two_spread(v, vx, lo, hi):
    low = iota((24, 128), 1) < 64
    turned = {b: pltpu.roll(v[b], 64, 1) for b in range(lo - 1, hi + 1)}
    for b in range(lo, hi):
        moved = (
            jnp.where(low, turned[b - 1], turned[b]),
            v[b],
            jnp.where(low, turned[b], turned[b + 1]),
        )
        for a, c in enumerate(moved):
            vx[3 * a, b], vx[3 * a + 2, b] = z_shifts(c, 64)
            vx[3 * a + 1, b] = c


def two_others(vx, c2, b):
    parts = []
    for a in range(3):
        total = None
        for c in range(3):
            plane = vx[3 * a + c, b]
            for s in range(3):
                k = 9 * a + 3 * s + c
                if k == 13:
                    continue
                moved = plane if s == 1 else pltpu.roll(plane, 1 if s == 0 else 23, 0)
                term = two_coefficient(c2, b - 1, k) * moved
                total = term if total is None else total + term
        parts.append(total)
    return parts[0] + parts[1] + parts[2]


def two_sweep(v, vx, w, g, c2, lo, hi):
    two_spread(v, vx, lo, hi)

    def compute(b):
        return KEEP * v[b] + w[b - 1] * (g[b - 1] - two_others(vx, c2, b))

    batch(lo, hi, hi - lo, compute, put(v))


def twice(step):
    lax.fori_loop(0, 2, lambda _, c: (step(), c)[1], 0)


def two_sources(g, own, ix):
    batch(0, 7, 7, lambda b: g[jnp.clip(ix + b - 3, 0, 15), 0:24], put(own))


def two_down(
    pos, g_all, c2lo, c2own, c2hi, g_out, v_out, v, vx, w, g, t
):
    ix, iy = pos[0], pos[1]
    c2 = (c2lo, c2own, c2hi)
    two_weights(w, c2, ix, iy)
    two_sources(g_all, g, ix)
    for b in (0, 8):
        v[b] = jnp.zeros((24, 128), F32)
    batch(1, 8, 7, lambda b: w[b - 1] * g[b - 1], put(v))
    twice(lambda: two_sweep(v, vx, w, g, c2, 2, 7))
    two_sweep(v, vx, w, g, c2, 3, 6)
    two_spread(v, vx, 3, 6)
    v_out[...] = v[4, 8:16]
    row_ok = rows_valid((24, 128), iy * 8 - 8, 128)

    def residual(b):
        rest = two_coefficient(c2, b - 1, 13) * v[b] + two_others(vx, c2, b)
        return jnp.where(row_ok & between(ix + b - 4, 16), g[b - 1] - rest, 0.0)

    batch(3, 6, 3, residual, put(v))
    low = iota((24, 128), 1) < 64
    here = 0.75 * v[4] + 0.25 * jnp.where(low, v[5], v[3])
    t[0] = dot(here, matrix(128, 128, lambda f, m: weight(f & 63, m & 31)))
    y = halve_rows(t, 0, 4)
    y = jnp.where(iota((4, 128), 1) >> 5 == iota((4, 128), 0), y, 0.0)
    g_out[...] = jnp.broadcast_to(jnp.sum(y, axis=0, keepdims=True), (8, 128))


def three_y(v, b):
    lane = iota((16, 128), 1)
    below = jnp.where(lane >= 32, pltpu.roll(v[b], 32, 1), pltpu.roll(v[b - 1], 32, 1))
    above = jnp.where(lane < 96, pltpu.roll(v[b], 96, 1), pltpu.roll(v[b + 1], 96, 1))
    return below, above


def three_x(c):
    row = iota((16, 128), 0)
    before = jnp.where(row > 0, pltpu.roll(c, 1, 0), 0.0)
    after = jnp.where(row < 15, pltpu.roll(c, 15, 0), 0.0)
    return before, after


def three_solve(v, vx, w, g, c3, iy):
    def coefficient(b, k):
        ref, index = c3[b]
        return ref[index, k]

    for b in (0, 8):
        v[b] = jnp.zeros((16, 128), F32)
    for b in range(7):
        ok = between(iy + b - 3, 16)
        w[b] = jnp.where(ok, RELAXATION / coefficient(b, 13), 0.0)
        v[b + 1] = w[b] * g[b]

    def spread(b):
        below, above = three_y(v, b)
        values = []
        for plane in (below, v[b], above):
            left, right = z_shifts(plane, 32)
            values += [left, plane, right]
        return values

    def keep(b, values):
        for k in range(9):
            vx[k, b - 1] = values[k]

    def update(b):
        parts = []
        for m in range(9):
            plane = vx[m, b - 1]
            before, after = three_x(plane)
            part = coefficient(b - 1, m) * before + coefficient(b - 1, 18 + m) * after
            if m != 4:
                part = part + coefficient(b - 1, 9 + m) * plane
            parts.append(part)
        rest = parts[0]
        for part in parts[1:]:
            rest = rest + part
        return KEEP * v[b] + w[b - 1] * (g[b - 1] - rest)

    def sweep(_, carry):
        batch(1, 8, 7, spread, keep)
        batch(1, 8, 7, update, put(v))
        return carry

    lax.fori_loop(0, 7, sweep, 0)


def coarse_up(
    pos, g3, v2, c3lo, c3own, c3hi, g2_all, c2lo, c2own, c2hi, g1, v1, v1lo, v1hi,
    cx, clo, chi, out,
    s3, vx3, w3, e, pc, s2, vx2, w2, g2, u, s1, vz, w1,
):
    ix, iy = pos[0], pos[1]
    c2 = (c2lo, c2own, c2hi)
    c3 = [(c3lo, 0), (c3lo, 1), (c3own, 0), (c3own, 1), (c3own, 2), (c3hi, 0), (c3hi, 1)]
    three_solve(s3, vx3, w3, g3, c3, iy)
    two_weights(w2, c2, ix, iy)
    two_sources(g2_all, g2, ix)
    one_weights(w1, cx, clo, chi, ix, iy)
    for b in range(3):
        for s, moved in enumerate(three_y(s3, b + 3)):
            c = 0.75 * s3[b + 3] + 0.25 * moved
            for p, beside in enumerate(three_x(c)):
                e[s, b, :, p * 128 : p * 128 + 128] = 0.75 * c + 0.25 * beside
    for q in range(4):

        def entry(r, m):
            same = (r >> 7 == m >> 6) & ((r >> 5) & 3 == q)
            return jnp.where(same, weight(m & 63, r & 31), 0.0)

        pz2 = matrix(256, 128, entry)
        for s in range(2):
            grown = dot(e[s].reshape(48, 256), pz2)
            for b in range(3):
                rows = pl.ds(8 * b + 2 * q + s, 16, stride=24)
                pc[rows, :] = grown[16 * b : 16 * b + 16]
    row_two = rows_valid((24, 128), iy * 8 - 8, 128)
    for j in range(9):
        ok = row_two & between(ix + j - 4, 16)
        x = jnp.clip(ix + j - 4, 0, 15)
        rows = pl.ds(pl.multiple_of(x * 24, 8), 24)
        s2[j] = jnp.where(ok, v2[x] + pc[rows, :], 0.0)
    for lo, hi in ((1, 8), (2, 7)):
        twice(lambda: two_sweep(s2, vx2, w2, g2, c2, lo, hi))
    low = iota((24, 128), 1) < 64
    for k in range(3):
        lo, here, hi = s2[k + 2], s2[k + 3], s2[k + 4]
        grow_rows(jnp.where(low, 0.75 * here, 0.25 * lo), u, 4 * k, 16)
        grow_rows(jnp.where(low, 0.75, 0.25) * here, u, 4 * k + 1, 16)
        grow_rows(jnp.where(low, 0.25, 0.75) * here, u, 4 * k + 2, 16)
        grow_rows(jnp.where(low, 0.25 * hi, 0.75 * here), u, 4 * k + 3, 16)
    row_one = rows_valid((32, 128), iy * 16 - 8, 256)
    pz1 = matrix(128, 128, lambda r, f: weight(f, r & 63))

    def add(p):
        ok = row_one & between(ix * 4 + p - 4, 64)
        held = jnp.concatenate([v1lo[p], v1[p], v1hi[p]], axis=0)
        return jnp.where(ok, held + dot(u[p], pz1), 0.0)

    for p in (0, 4, 8):
        batch(p, p + 4, 4, add, put(s1))

    def update(p):
        rest = one_others(vz, cx, clo, chi, p, p)
        return KEEP * s1[p] + w1[p] * (g1[p + 1] - rest)

    for k in range(4):
        one_spread(s1, vz, k, 12 - k)
        batch(1 + k, 11 - k, 2, update, put(s1))
    for p in range(4):
        out[p] = s1[p + 4, 8:24]


def vm(*shape):
    return pltpu.VMEM(shape, F32)


def call(kernel, name, outs, scratch, pos, *operands):
    shapes = [jax.ShapeDtypeStruct(s, F32) for s in outs]
    return pl.pallas_call(
        kernel,
        name=name,
        out_shape=shapes,
        in_specs=[pl.BlockSpec(memory_space=pltpu.SMEM)]
        + [pl.BlockSpec(memory_space=pltpu.VMEM)] * len(operands),
        out_specs=[pl.BlockSpec(memory_space=pltpu.VMEM)] * len(outs),
        scratch_shapes=scratch,
        compiler_params=pltpu.CompilerParams(vmem_limit_bytes=50 * 2**20),
    )(pos, *operands)


def both(value, axis, dim, width):
    length = value.shape[dim]
    last = lax.slice_in_dim(value, length - width, length, axis=dim)
    first = lax.slice_in_dim(value, 0, width, axis=dim)
    return ring(last, axis, 1), ring(first, axis, -1)


def wide(value, axis, dim, width):
    before, after = both(value, axis, dim, width)
    return jnp.concatenate([before, value, after], axis=dim)


def after_all(value, *others):
    return lax.optimization_barrier((value,) + others)[0]


def on_device(source, damping, coarse_one, coarse_two, coarse_three):
    pos = jnp.stack([lax.axis_index("gx"), lax.axis_index("gy")]).astype(jnp.int32)

    with jax.named_scope("fine_halo"):
        last = jnp.stack([source[1:], damping[1:]])
        first = jnp.stack([source[:7], damping[:7]])
        xlo, xhi = ring(last, "gx", 1), ring(first, "gx", -1)

    with jax.named_scope("two_three_halo"):
        coarse_two, coarse_three, one = lax.optimization_barrier(
            (coarse_two, coarse_three, coarse_one, last, first)
        )[:3]
        c2 = jnp.concatenate([coarse_two[:, 0], coarse_two[:, 1]], axis=-1).reshape(216, 128)
        c3 = jnp.concatenate([coarse_three[:, 0, i] for i in range(4)], axis=-1)
        load = jnp.concatenate([one.reshape(1728, 128), c2])
        xb, xa = ring(load, "gx", 1), ring(load, "gx", -1)

    with jax.named_scope("fine_halo"):
        edge = []
        for rows in (slice(24, 32), slice(0, 8)):
            mid = jnp.stack([source[:, rows], damping[:, rows]])
            edge.append(jnp.concatenate([xlo[:, :, rows], mid, xhi[:, :, rows]], axis=1))
        ylo, yhi = ring(edge[0], "gy", 1), ring(edge[1], "gy", -1)
        yb, ya = both(after_all(coarse_one, *edge), "gy", 2, 8)

    with jax.named_scope("fine_down"):
        v0, g1, s0, w0 = call(
            fine_down, "fine_down",
            [(16, 48, 256), (6, 16, 128), (16, 48, 256), (16, 48, 256)],
            [vm(22, 48, 256)] * 4 + [vm(6, 48, 128)],
            pos, source, damping, xlo, xhi, ylo, yhi,
        )

    with jax.named_scope("one_halo"):
        xb, xa, yb, ya, g1 = lax.optimization_barrier((xb, xa, yb, ya, g1))

    with jax.named_scope("one_exchange"):
        at = 13 * 64
        edge_lo = RELAXATION * g1[0:1] / xb[at + 48 : at + 64].reshape(1, 16, 128)
        edge_hi = RELAXATION * g1[5:6] / xa[at : at + 16].reshape(1, 16, 128)
        up = jnp.concatenate([edge_lo, g1[1:5]])
        down = jnp.concatenate([g1[1:5], edge_hi])
        before, after = ring(up, "gx", 1), ring(down, "gx", -1)
        xb, xa = lax.optimization_barrier((xb, xa, up, down))[:2]
        cxlo, cxhi = xb[:1728].reshape(27, 4, 16, 128), xa[:1728].reshape(27, 4, 16, 128)
        tlo, thi = xb[1728:], xa[1728:]
        one_lo, one_hi = yb, ya
        sides = jnp.concatenate([cxlo, cxhi], axis=1)
        g1x = jnp.concatenate([before, g1[1:5], after])
        rows = [slice(8, 16), slice(0, 8)]
        up, down = [
            jnp.concatenate([sides[:, :, r].reshape(1728, 128), g1x[:, r].reshape(112, 128)])
            for r in rows
        ]
        up, down = ring(up, "gy", 1), ring(down, "gy", -1)
        g1e = jnp.concatenate(
            [up[1728:].reshape(14, 8, 128), g1x, down[1728:].reshape(14, 8, 128)], axis=1
        )
        side_lo, side_hi = [p[:1728].reshape(27, 8, 8, 128) for p in (up, down)]

    with jax.named_scope("two_halo"):
        tlo, thi = lax.optimization_barrier((tlo, thi, before, after))[:2]
        far_lo = ring(jnp.stack([c2, thi]), "gx", 3)
        far_hi = ring(jnp.stack([tlo, c2]), "gx", -3)
        far_lo, far_hi = lax.optimization_barrier((far_lo, far_hi, g1e))[:2]
        c2own = jnp.concatenate([far_lo, tlo[None], c2[None], thi[None], far_hi])
        c2lo, c2hi = ring(c2own, "gy", 1), ring(c2own, "gy", -1)

    with jax.named_scope("one_down"):
        cx = jnp.concatenate([after_all(cxlo, before), coarse_one, cxhi], axis=1)
        clo = jnp.concatenate([side_lo[:, :4], one_lo, side_lo[:, 4:]], axis=1)
        chi = jnp.concatenate([side_hi[:, :4], one_hi, side_hi[:, 4:]], axis=1)
        g2, v1 = call(
            one_down, "one_down", [(8, 128), (4, 16, 128)],
            [vm(14, 32, 128), vm(3, 14, 32, 128), vm(12, 32, 128), vm(2, 32, 128)],
            pos, g1e, cx, clo, chi,
        )

    with jax.named_scope("two_exchange"):
        load = jnp.concatenate([wide(g2, "gy", 0, 8), jnp.pad(c3, ((0, 5), (0, 0)))])
        load, c2lo, c2hi = lax.optimization_barrier((load, c2lo, c2hi))
        g2e = everyone(load, "gx")

    with jax.named_scope("three_halo"):
        c3x = jnp.transpose(g2e[:, 24:51], (1, 0, 2)).reshape(432, 128)
        three_lo, three_hi = ring(c3x, "gy", 1), ring(c3x, "gy", -1)

    with jax.named_scope("one_values"):
        v1b, v1a = both(v1, "gx", 0, 4)

    with jax.named_scope("two_down"):
        g3, v2 = call(
            two_down, "two_down", [(8, 128), (8, 128)],
            [
                vm(9, 24, 128), vm(9, 9, 24, 128), vm(7, 24, 128), vm(7, 24, 128),
                vm(1, 24, 128),
            ],
            pos, g2e, c2lo, c2own, c2hi,
        )

    with jax.named_scope("three_exchange"):
        v1b, v1a = lax.optimization_barrier((v1b, v1a, g3))[:2]
        v1 = jnp.concatenate([v1b, v1, v1a])
        up = jnp.concatenate([g3, v2, v1[:, 8:].reshape(96, 128)])
        down = jnp.concatenate([g3, v2, v1[:, :8].reshape(96, 128)])
        before, after = ring(up, "gy", 1), ring(down, "gy", -1)
        v1lo, v1hi = before[16:].reshape(12, 8, 128), after[16:].reshape(12, 8, 128)
        three_lo, three_hi, before, after = lax.optimization_barrier(
            (three_lo, three_hi, before, after)
        )
        c3own = jnp.stack([three_lo, c3x, three_hi]).reshape(3, 27, 16, 128)
        trip = jnp.concatenate([before[:1], g3[:1], after[:1]])
        far_before, far_after = ring(trip, "gy", 2), ring(trip, "gy", -2)
        c3up, c3down = c3own[:2].reshape(864, 128), c3own[1:].reshape(864, 128)
        g3, c3up, c3down = lax.optimization_barrier((g3, c3up, c3down))
        c3lo = ring(c3up, "gy", 2).reshape(2, 27, 16, 128)
        c3hi = ring(c3down, "gy", -2).reshape(2, 27, 16, 128)
        gv = everyone(
            jnp.concatenate(
                [far_before[:2], trip, far_after[1:], g3[:1], before[8:16], v2, after[8:16]]
            ),
            "gx",
        )
        g3e, v2e = jnp.transpose(gv[:, :7], (1, 0, 2)), gv[:, 8:]

    with jax.named_scope("coarse_up"):
        (c1,) = call(
            coarse_up, "coarse_up", [(4, 16, 128)],
            [
                vm(9, 16, 128), vm(9, 7, 16, 128), vm(7, 16, 128), vm(2, 3, 16, 256),
                vm(384, 128),
                vm(9, 24, 128), vm(9, 9, 24, 128), vm(7, 24, 128), vm(7, 24, 128),
                vm(12, 32, 128), vm(12, 32, 128), vm(3, 12, 32, 128), vm(12, 32, 128),
            ],
            pos, g3e, v2e, c3lo, c3own, c3hi, g2e, c2lo, c2own, c2hi, g1e, v1, v1lo, v1hi, cx, clo, chi,
        )

    with jax.named_scope("one_back"):
        c1e = wide(wide(c1, "gx", 0, 3), "gy", 1, 8)

    with jax.named_scope("fine_up"):
        (out,) = call(
            fine_up, "fine_up", [(8, 32, 256)],
            [vm(16, 48, 256)] * 2 + [vm(10, 48, 128)], pos, s0, w0, v0, c1e,
        )
    return out


def solution(mesh):
    in_specs = (
        P("gx", "gy", None),
        P("gx", "gy", None),
        P(None, "gx", "gy", None),
        P(None, "gx", "gy", None),
        P(None, "gx", "gy", None),
    )
    return jax.shard_map(
        on_device, mesh=mesh, in_specs=in_specs, out_specs=P("gx", "gy", None), check_vma=False
    )
```

```python
import jax
import jax.numpy as jnp
from jax import lax
from jax.experimental import pallas as pl
from jax.experimental.pallas import tpu as pltpu
from jax.sharding import PartitionSpec as P

F32 = jnp.float32
RELAXATION = 0.8
KEEP = 1.0 - RELAXATION
N = 16
HI = lax.Precision.HIGHEST


def ring(value, axis, step):
    return lax.ppermute(value, axis, [(i, (i + step) % N) for i in range(N)])


def everyone(block, axis):
    copies = jnp.broadcast_to(block[None], (N,) + block.shape)
    return lax.all_to_all(copies, axis, 0, 0)


def iota(shape, dim):
    return lax.broadcasted_iota(jnp.int32, shape, dim)


def weight(fine, coarse):
    d = fine - 2 * coarse
    return jnp.where((d == 0) | (d == 1), 0.75, jnp.where((d == -1) | (d == 2), 0.25, 0.0))


def matrix(rows, lanes, entry):
    return entry(iota((rows, lanes), 0), iota((rows, lanes), 1)).astype(F32)


def dot(a, b):
    return jnp.dot(a, b, precision=HI, preferred_element_type=F32)


def batch(lo, hi, group, compute, store):
    def some(indices):
        for i, value in [(i, compute(i)) for i in indices]:
            store(i, value)

    count = (hi - lo) // group
    if count == 1:
        some(range(lo, lo + group))
    elif count > 1:
        lax.fori_loop(
            0, count, lambda n, c: (some([lo + n * group + i for i in range(group)]), c)[1], 0
        )
    if lo + count * group < hi:
        some(range(lo + count * group, hi))


def put(ref):
    def store(i, value):
        ref[i] = value

    return store


def rows_valid(shape, first, count):
    row = iota(shape, 0) + first
    return (row >= 0) & (row < count)


def between(i, count):
    return (i >= 0) & (i < count)


def z_shifts(c, period):
    lane = iota(c.shape, 1) & (period - 1)
    size = c.shape[1]
    below = jnp.where(lane > 0, pltpu.roll(c, 1, 1), 0.0)
    above = jnp.where(lane < period - 1, pltpu.roll(c, size - 1, 1), 0.0)
    return below, above


def grow_rows(coarse, ref, index, count):
    mid = 0.75 * coarse[4 : 4 + count]
    ref[index, pl.ds(0, count, stride=2), :] = mid + 0.25 * coarse[3 : 3 + count]
    ref[index, pl.ds(1, count, stride=2), :] = mid + 0.25 * coarse[5 : 5 + count]


def halve_rows(ref, index, count):
    part = [ref[index, pl.ds(7 + i, count, stride=2), :] for i in range(4)]
    return 0.25 * (part[0] + part[3]) + 0.75 * (part[1] + part[2])


def six(before, c, after):
    rows = c.shape[0]
    below, above = z_shifts(c, c.shape[1])
    return before + after + pltpu.roll(c, 1, 0) + pltpu.roll(c, rows - 1, 0) + below + above


def fine_down(
    pos, source, damping, xlo, xhi, ylo, yhi, v_out, g_out, s_out, w_out, a, b, s, w, t
):
    ix, iy = pos[0], pos[1]
    row_ok = rows_valid((48, 256), iy * 32 - 8, 512)

    def start(lo, hi, s_mid, d_mid):
        def compute(p):
            ok = row_ok & between(ix * 8 + p - 7, 128)
            rows = jnp.concatenate([ylo[0, p], s_mid(p - lo), yhi[0, p]], axis=0)
            damp = jnp.concatenate([ylo[1, p], d_mid(p - lo), yhi[1, p]], axis=0)
            return rows, jnp.where(ok, RELAXATION / (6.0 + damp), 0.0)

        def store(p, value):
            s[p], w[p] = value
            a[p] = value[0] * value[1]

        batch(lo, hi, 1, compute, store)

    start(0, 7, lambda i: xlo[0, i], lambda i: xlo[1, i])
    start(7, 15, lambda i: source[i], lambda i: damping[i])
    start(15, 22, lambda i: xhi[0, i], lambda i: xhi[1, i])

    def sweep(src, dst, lo, hi, off):
        def compute(p):
            c = src[p]
            return KEEP * c + w[p] * (s[p] + six(src[p - 1], c, src[p + 1]))

        def store(p, value):
            dst[p - off] = value

        batch(lo, hi, 2, compute, store)

    sweep(a, b, 1, 21, 0)
    sweep(b, a, 2, 20, 0)
    sweep(a, v_out, 3, 19, 3)

    def residual(mid, first):
        def compute(p):
            ok = row_ok & between(ix * 8 + p - 7, 128)
            damp = jnp.concatenate([ylo[1, p], mid(p - first), yhi[1, p]], axis=0)
            c = v_out[p - 3]
            r = s[p] + six(v_out[p - 4], c, v_out[p - 2]) - (6.0 + damp) * c
            return jnp.where(ok, r, 0.0)

        return compute

    batch(4, 7, 3, residual(lambda i: xlo[1, i], 0), put(b))
    batch(7, 15, 2, residual(lambda i: damping[i], 7), put(b))
    batch(15, 18, 3, residual(lambda i: xhi[1, i], 15), put(b))
    s_out[...] = s[3:19]
    w_out[...] = w[3:19]

    rz = matrix(256, 128, weight)

    def coarse(j):
        q = 2 * j + 4
        return dot(0.25 * (b[q] + b[q + 3]) + 0.75 * (b[q + 1] + b[q + 2]), rz)

    batch(0, 6, 6, coarse, put(t))
    batch(0, 6, 6, lambda j: halve_rows(t, j, 16), put(g_out))


def fine_up(pos, s, w, v_in, c1, out, a, b, u):
    ix, iy = pos[0], pos[1]
    row_ok = rows_valid((48, 256), iy * 32 - 8, 512)
    coarse_ok = rows_valid((32, 128), iy * 16 - 8, 256)
    for q in range(10):
        ok = coarse_ok & between(ix * 4 + q - 3, 64)
        grow_rows(jnp.where(ok, c1[q], 0.0), u, q, 24)

    pz = matrix(128, 256, lambda j, f: weight(f, j))

    def add(f):
        ok = row_ok & between(ix * 8 + f - 4, 128)
        h = f // 2
        fine = dot(0.75 * u[h + 1] + 0.25 * u[h + 2 * (f % 2)], pz)
        return v_in[f] + jnp.where(ok, fine, 0.0)

    for h in range(0, 16, 4):
        batch(h, h + 4, 4, add, put(a))

    def sweep(src, dst, lo, hi, keep_rows):
        def compute(p):
            c = src[p]
            return KEEP * c + w[p] * (s[p] + six(src[p - 1], c, src[p + 1]))

        def store(p, value):
            if keep_rows:
                dst[p - lo] = value[8:40]
            else:
                dst[p] = value

        batch(lo, hi, 2, compute, store)

    sweep(a, b, 1, 15, False)
    sweep(b, a, 2, 14, False)
    sweep(a, b, 3, 13, False)
    sweep(b, out, 4, 12, True)


def one_coefficient(cx, clo, chi, k, p):
    return jnp.concatenate([clo[k, p], cx[k, p], chi[k, p]], axis=0)


def one_weights(w, cx, clo, chi, ix, iy):
    def compute(p):
        ok = rows_valid((32, 128), iy * 16 - 8, 256) & between(ix * 4 + p - 4, 64)
        return jnp.where(ok, RELAXATION / one_coefficient(cx, clo, chi, 13, p), 0.0)

    batch(0, 12, 4, compute, put(w))


def one_spread(v, vz, lo, hi):
    def compute(p):
        c = v[p]
        below, above = z_shifts(c, 128)
        return below, c, above

    def store(p, value):
        for i in range(3):
            vz[i, p] = value[i]

    batch(lo, hi, 4, compute, store)


def one_others(vz, cx, clo, chi, p, cp):
    parts = []
    for a in range(3):
        total = None
        for c in range(3):
            plane = vz[c, p + a - 1]
            for b in range(3):
                k = 9 * a + 3 * b + c
                if k == 13:
                    continue
                moved = plane if b == 1 else pltpu.roll(plane, 1 if b == 0 else 31, 0)
                term = one_coefficient(cx, clo, chi, k, cp) * moved
                total = term if total is None else total + term
        parts.append(total)
    return parts[0] + parts[1] + parts[2]


def one_down(pos, g, cx, clo, chi, g_out, v_out, v, vz, w, t):
    ix, iy = pos[0], pos[1]
    one_weights(w, cx, clo, chi, ix, iy)
    row_ok = rows_valid((32, 128), iy * 16 - 8, 256)
    for p in (0, 13):
        v[p] = jnp.where(row_ok & between(ix * 4 + p - 5, 64), g[p], 0.0)
    batch(1, 13, 4, lambda p: w[p - 1] * g[p], put(v))

    def update(p):
        rest = one_others(vz, cx, clo, chi, p, p - 1)
        return KEEP * v[p] + w[p - 1] * (g[p] - rest)

    for k in range(3):
        one_spread(v, vz, k, 14 - k)
        batch(1 + k, 13 - k, 2, update, put(v))
    one_spread(v, vz, 3, 11)

    def residual(p):
        ok = row_ok & between(ix * 4 + p - 5, 64)
        rest = one_others(vz, cx, clo, chi, p, p - 1)
        own = one_coefficient(cx, clo, chi, 13, p - 1) * vz[1, p]
        return jnp.where(ok, g[p] - own - rest, 0.0)

    batch(4, 10, 2, residual, put(v))
    for p in range(4):
        v_out[p] = vz[1, p + 5, 8:24]
    total = None
    for j in range(2):
        q = 2 * j + 4
        t[j] = 0.25 * (v[q] + v[q + 3]) + 0.75 * (v[q + 1] + v[q + 2])
    for j in range(2):
        rz = matrix(128, 128, lambda f, m: jnp.where(m >> 6 == j, weight(f, m & 63), 0.0))
        term = dot(halve_rows(t, j, 8), rz)
        total = term if total is None else total + term
    g_out[...] = total


def two_coefficient(c2, block, k):
    return jnp.concatenate([ref[block, pl.ds(k * 8, 8), :] for ref in c2], axis=0)


def two_weights(w, c2, ix, iy):
    row_ok = rows_valid((24, 128), iy * 8 - 8, 128)

    def compute(b):
        ok = row_ok & between(ix + b - 3, 16)
        return jnp.where(ok, RELAXATION / two_coefficient(c2, b, 13), 0.0)

    batch(0, 7, 7, compute, put(w))


def two_spread(v, vx, lo, hi):
    low = iota((24, 128), 1) < 64
    turned = {b: pltpu.roll(v[b], 64, 1) for b in range(lo - 1, hi + 1)}
    for b in range(lo, hi):
        moved = (
            jnp.where(low, turned[b - 1], turned[b]),
            v[b],
            jnp.where(low, turned[b], turned[b + 1]),
        )
        for a, c in enumerate(moved):
            vx[3 * a, b], vx[3 * a + 2, b] = z_shifts(c, 64)
            vx[3 * a + 1, b] = c


def two_others(vx, c2, b):
    parts = []
    for a in range(3):
        total = None
        for c in range(3):
            plane = vx[3 * a + c, b]
            for s in range(3):
                k = 9 * a + 3 * s + c
                if k == 13:
                    continue
                moved = plane if s == 1 else pltpu.roll(plane, 1 if s == 0 else 23, 0)
                term = two_coefficient(c2, b - 1, k) * moved
                total = term if total is None else total + term
        parts.append(total)
    return parts[0] + parts[1] + parts[2]


def two_sweep(v, vx, w, g, c2, lo, hi):
    two_spread(v, vx, lo, hi)

    def compute(b):
        return KEEP * v[b] + w[b - 1] * (g[b - 1] - two_others(vx, c2, b))

    batch(lo, hi, hi - lo, compute, put(v))


def twice(step):
    lax.fori_loop(0, 2, lambda _, c: (step(), c)[1], 0)


def two_sources(g, own, ix):
    batch(0, 7, 7, lambda b: g[jnp.clip(ix + b - 3, 0, 15), 0:24], put(own))


def two_down(
    pos, g_all, c2lo, c2own, c2hi, g_out, v_out, v, vx, w, g, t
):
    ix, iy = pos[0], pos[1]
    c2 = (c2lo, c2own, c2hi)
    two_weights(w, c2, ix, iy)
    two_sources(g_all, g, ix)
    for b in (0, 8):
        v[b] = jnp.zeros((24, 128), F32)
    batch(1, 8, 7, lambda b: w[b - 1] * g[b - 1], put(v))
    twice(lambda: two_sweep(v, vx, w, g, c2, 2, 7))
    two_sweep(v, vx, w, g, c2, 3, 6)
    two_spread(v, vx, 3, 6)
    v_out[...] = v[4, 8:16]
    row_ok = rows_valid((24, 128), iy * 8 - 8, 128)

    def residual(b):
        rest = two_coefficient(c2, b - 1, 13) * v[b] + two_others(vx, c2, b)
        return jnp.where(row_ok & between(ix + b - 4, 16), g[b - 1] - rest, 0.0)

    batch(3, 6, 3, residual, put(v))
    low = iota((24, 128), 1) < 64
    here = 0.75 * v[4] + 0.25 * jnp.where(low, v[5], v[3])
    t[0] = dot(here, matrix(128, 128, lambda f, m: weight(f & 63, m & 31)))
    y = halve_rows(t, 0, 4)
    y = jnp.where(iota((4, 128), 1) >> 5 == iota((4, 128), 0), y, 0.0)
    g_out[...] = jnp.broadcast_to(jnp.sum(y, axis=0, keepdims=True), (8, 128))


def three_y(v, b):
    lane = iota((16, 128), 1)
    below = jnp.where(lane >= 32, pltpu.roll(v[b], 32, 1), pltpu.roll(v[b - 1], 32, 1))
    above = jnp.where(lane < 96, pltpu.roll(v[b], 96, 1), pltpu.roll(v[b + 1], 96, 1))
    return below, above


def three_x(c):
    row = iota((16, 128), 0)
    before = jnp.where(row > 0, pltpu.roll(c, 1, 0), 0.0)
    after = jnp.where(row < 15, pltpu.roll(c, 15, 0), 0.0)
    return before, after


def three_solve(v, vx, w, g, c3, iy):
    def coefficient(b, k):
        ref, index = c3[b]
        return ref[index, k]

    for b in (0, 8):
        v[b] = jnp.zeros((16, 128), F32)
    for b in range(7):
        ok = between(iy + b - 3, 16)
        w[b] = jnp.where(ok, RELAXATION / coefficient(b, 13), 0.0)
        v[b + 1] = w[b] * g[b]

    def spread(b):
        below, above = three_y(v, b)
        values = []
        for plane in (below, v[b], above):
            left, right = z_shifts(plane, 32)
            values += [left, plane, right]
        return values

    def keep(b, values):
        for k in range(9):
            vx[k, b - 1] = values[k]

    def update(b):
        parts = []
        for m in range(9):
            plane = vx[m, b - 1]
            before, after = three_x(plane)
            part = coefficient(b - 1, m) * before + coefficient(b - 1, 18 + m) * after
            if m != 4:
                part = part + coefficient(b - 1, 9 + m) * plane
            parts.append(part)
        rest = parts[0]
        for part in parts[1:]:
            rest = rest + part
        return KEEP * v[b] + w[b - 1] * (g[b - 1] - rest)

    def sweep(_, carry):
        batch(1, 8, 7, spread, keep)
        batch(1, 8, 7, update, put(v))
        return carry

    lax.fori_loop(0, 7, sweep, 0)


def coarse_up(
    pos, g3, v2, c3lo, c3own, c3hi, g2_all, c2lo, c2own, c2hi, g1, v1, v1lo, v1hi,
    cx, clo, chi, out,
    s3, vx3, w3, e, pc, s2, vx2, w2, g2, u, s1, vz, w1,
):
    ix, iy = pos[0], pos[1]
    c2 = (c2lo, c2own, c2hi)
    c3 = [(c3lo, 0), (c3lo, 1), (c3own, 0), (c3own, 1), (c3own, 2), (c3hi, 0), (c3hi, 1)]
    three_solve(s3, vx3, w3, g3, c3, iy)
    two_weights(w2, c2, ix, iy)
    two_sources(g2_all, g2, ix)
    one_weights(w1, cx, clo, chi, ix, iy)
    for b in range(3):
        for s, moved in enumerate(three_y(s3, b + 3)):
            c = 0.75 * s3[b + 3] + 0.25 * moved
            for p, beside in enumerate(three_x(c)):
                e[s, b, :, p * 128 : p * 128 + 128] = 0.75 * c + 0.25 * beside
    for q in range(4):

        def entry(r, m):
            same = (r >> 7 == m >> 6) & ((r >> 5) & 3 == q)
            return jnp.where(same, weight(m & 63, r & 31), 0.0)

        pz2 = matrix(256, 128, entry)
        for s in range(2):
            grown = dot(e[s].reshape(48, 256), pz2)
            for b in range(3):
                rows = pl.ds(8 * b + 2 * q + s, 16, stride=24)
                pc[rows, :] = grown[16 * b : 16 * b + 16]
    row_two = rows_valid((24, 128), iy * 8 - 8, 128)
    for j in range(9):
        ok = row_two & between(ix + j - 4, 16)
        x = jnp.clip(ix + j - 4, 0, 15)
        rows = pl.ds(pl.multiple_of(x * 24, 8), 24)
        s2[j] = jnp.where(ok, v2[x] + pc[rows, :], 0.0)
    for lo, hi in ((1, 8), (2, 7)):
        twice(lambda: two_sweep(s2, vx2, w2, g2, c2, lo, hi))
    low = iota((24, 128), 1) < 64
    for k in range(3):
        lo, here, hi = s2[k + 2], s2[k + 3], s2[k + 4]
        grow_rows(jnp.where(low, 0.75 * here, 0.25 * lo), u, 4 * k, 16)
        grow_rows(jnp.where(low, 0.75, 0.25) * here, u, 4 * k + 1, 16)
        grow_rows(jnp.where(low, 0.25, 0.75) * here, u, 4 * k + 2, 16)
        grow_rows(jnp.where(low, 0.25 * hi, 0.75 * here), u, 4 * k + 3, 16)
    row_one = rows_valid((32, 128), iy * 16 - 8, 256)
    pz1 = matrix(128, 128, lambda r, f: weight(f, r & 63))

    def add(p):
        ok = row_one & between(ix * 4 + p - 4, 64)
        held = jnp.concatenate([v1lo[p], v1[p], v1hi[p]], axis=0)
        return jnp.where(ok, held + dot(u[p], pz1), 0.0)

    for p in (0, 4, 8):
        batch(p, p + 4, 4, add, put(s1))

    def update(p):
        rest = one_others(vz, cx, clo, chi, p, p)
        return KEEP * s1[p] + w1[p] * (g1[p + 1] - rest)

    for k in range(4):
        one_spread(s1, vz, k, 12 - k)
        batch(1 + k, 11 - k, 2, update, put(s1))
    for p in range(4):
        out[p] = s1[p + 4, 8:24]


def vm(*shape):
    return pltpu.VMEM(shape, F32)


def call(kernel, name, outs, scratch, pos, *operands):
    shapes = [jax.ShapeDtypeStruct(s, F32) for s in outs]
    return pl.pallas_call(
        kernel,
        name=name,
        out_shape=shapes,
        in_specs=[pl.BlockSpec(memory_space=pltpu.SMEM)]
        + [pl.BlockSpec(memory_space=pltpu.VMEM)] * len(operands),
        out_specs=[pl.BlockSpec(memory_space=pltpu.VMEM)] * len(outs),
        scratch_shapes=scratch,
        compiler_params=pltpu.CompilerParams(vmem_limit_bytes=50 * 2**20),
    )(pos, *operands)


def both(value, axis, dim, width):
    length = value.shape[dim]
    last = lax.slice_in_dim(value, length - width, length, axis=dim)
    first = lax.slice_in_dim(value, 0, width, axis=dim)
    return ring(last, axis, 1), ring(first, axis, -1)


def wide(value, axis, dim, width):
    before, after = both(value, axis, dim, width)
    return jnp.concatenate([before, value, after], axis=dim)


def after_all(value, *others):
    return lax.optimization_barrier((value,) + others)[0]


def on_device(source, damping, coarse_one, coarse_two, coarse_three):
    pos = jnp.stack([lax.axis_index("gx"), lax.axis_index("gy")]).astype(jnp.int32)

    with jax.named_scope("fine_halo"):
        last = jnp.stack([source[1:], damping[1:]])
        first = jnp.stack([source[:7], damping[:7]])
        xlo, xhi = ring(last, "gx", 1), ring(first, "gx", -1)

    with jax.named_scope("two_three_halo"):
        coarse_two, coarse_three, one = lax.optimization_barrier(
            (coarse_two, coarse_three, coarse_one, last, first)
        )[:3]
        c2 = jnp.concatenate([coarse_two[:, 0], coarse_two[:, 1]], axis=-1).reshape(216, 128)
        c3 = jnp.concatenate([coarse_three[:, 0, i] for i in range(4)], axis=-1)
        load = jnp.concatenate([one.reshape(1728, 128), c2])
        xb, xa = ring(load, "gx", 1), ring(load, "gx", -1)

    with jax.named_scope("fine_halo"):
        edge = []
        for rows in (slice(24, 32), slice(0, 8)):
            mid = jnp.stack([source[:, rows], damping[:, rows]])
            edge.append(jnp.concatenate([xlo[:, :, rows], mid, xhi[:, :, rows]], axis=1))
        ylo, yhi = ring(edge[0], "gy", 1), ring(edge[1], "gy", -1)
        yb, ya = both(after_all(coarse_one, *edge), "gy", 2, 8)

    with jax.named_scope("fine_down"):
        v0, g1, s0, w0 = call(
            fine_down, "fine_down",
            [(16, 48, 256), (6, 16, 128), (16, 48, 256), (16, 48, 256)],
            [vm(22, 48, 256)] * 4 + [vm(6, 48, 128)],
            pos, source, damping, xlo, xhi, ylo, yhi,
        )

    with jax.named_scope("one_halo"):
        xb, xa, yb, ya, g1 = lax.optimization_barrier((xb, xa, yb, ya, g1))

    with jax.named_scope("one_exchange"):
        at = 13 * 64
        edge_lo = RELAXATION * g1[0:1] / xb[at + 48 : at + 64].reshape(1, 16, 128)
        edge_hi = RELAXATION * g1[5:6] / xa[at : at + 16].reshape(1, 16, 128)
        up = jnp.concatenate([edge_lo, g1[1:5]])
        down = jnp.concatenate([g1[1:5], edge_hi])
        before, after = ring(up, "gx", 1), ring(down, "gx", -1)
        xb, xa = lax.optimization_barrier((xb, xa, up, down))[:2]
        cxlo, cxhi = xb[:1728].reshape(27, 4, 16, 128), xa[:1728].reshape(27, 4, 16, 128)
        tlo, thi = xb[1728:], xa[1728:]
        one_lo, one_hi = yb, ya
        sides = jnp.concatenate([cxlo, cxhi], axis=1)
        g1x = jnp.concatenate([before, g1[1:5], after])
        rows = [slice(8, 16), slice(0, 8)]
        up, down = [
            jnp.concatenate([sides[:, :, r].reshape(1728, 128), g1x[:, r].reshape(112, 128)])
            for r in rows
        ]
        up, down = ring(up, "gy", 1), ring(down, "gy", -1)
        g1e = jnp.concatenate(
            [up[1728:].reshape(14, 8, 128), g1x, down[1728:].reshape(14, 8, 128)], axis=1
        )
        side_lo, side_hi = [p[:1728].reshape(27, 8, 8, 128) for p in (up, down)]

    with jax.named_scope("two_halo"):
        tlo, thi = lax.optimization_barrier((tlo, thi, before, after))[:2]
        far_lo = ring(jnp.stack([c2, thi]), "gx", 3)
        far_hi = ring(jnp.stack([tlo, c2]), "gx", -3)

    with jax.named_scope("one_down"):
        cx = jnp.concatenate([after_all(cxlo, before), coarse_one, cxhi], axis=1)
        clo = jnp.concatenate([side_lo[:, :4], one_lo, side_lo[:, 4:]], axis=1)
        chi = jnp.concatenate([side_hi[:, :4], one_hi, side_hi[:, 4:]], axis=1)
        g2, v1 = call(
            one_down, "one_down", [(8, 128), (4, 16, 128)],
            [vm(14, 32, 128), vm(3, 14, 32, 128), vm(12, 32, 128), vm(2, 32, 128)],
            pos, g1e, cx, clo, chi,
        )

    with jax.named_scope("two_exchange"):
        load = jnp.concatenate([wide(g2, "gy", 0, 8), jnp.pad(c3, ((0, 5), (0, 0)))])
        far_lo, far_hi = lax.optimization_barrier((far_lo, far_hi, g2))[:2]
        c2own = jnp.concatenate([far_lo, tlo[None], c2[None], thi[None], far_hi])
        c2lo, c2hi = ring(c2own, "gy", 1), ring(c2own, "gy", -1)
        load = after_all(load, c2own)
        g2e = everyone(load, "gx")

    with jax.named_scope("three_halo"):
        c3x = jnp.transpose(g2e[:, 24:51], (1, 0, 2)).reshape(432, 128)
        three_lo, three_hi = ring(c3x, "gy", 1), ring(c3x, "gy", -1)

    with jax.named_scope("one_values"):
        v1b, v1a = both(v1, "gx", 0, 4)

    with jax.named_scope("two_down"):
        g3, v2 = call(
            two_down, "two_down", [(8, 128), (8, 128)],
            [
                vm(9, 24, 128), vm(9, 9, 24, 128), vm(7, 24, 128), vm(7, 24, 128),
                vm(1, 24, 128),
            ],
            pos, g2e, c2lo, c2own, c2hi,
        )

    with jax.named_scope("three_exchange"):
        v1b, v1a = lax.optimization_barrier((v1b, v1a, g3))[:2]
        v1 = jnp.concatenate([v1b, v1, v1a])
        up = jnp.concatenate([g3, v2, v1[:, 8:].reshape(96, 128)])
        down = jnp.concatenate([g3, v2, v1[:, :8].reshape(96, 128)])
        before, after = ring(up, "gy", 1), ring(down, "gy", -1)
        v1lo, v1hi = before[16:].reshape(12, 8, 128), after[16:].reshape(12, 8, 128)
        three_lo, three_hi, before, after = lax.optimization_barrier(
            (three_lo, three_hi, before, after)
        )
        c3own = jnp.stack([three_lo, c3x, three_hi]).reshape(3, 27, 16, 128)
        trip = jnp.concatenate([before[:1], g3[:1], after[:1]])
        far_before, far_after = ring(trip, "gy", 2), ring(trip, "gy", -2)
        c3up, c3down = c3own[:2].reshape(864, 128), c3own[1:].reshape(864, 128)
        g3, c3up, c3down = lax.optimization_barrier((g3, c3up, c3down))
        c3lo = ring(c3up, "gy", 2).reshape(2, 27, 16, 128)
        c3hi = ring(c3down, "gy", -2).reshape(2, 27, 16, 128)
        gv = everyone(
            jnp.concatenate(
                [far_before[:2], trip, far_after[1:], g3[:1], before[8:16], v2, after[8:16]]
            ),
            "gx",
        )
        g3e, v2e = jnp.transpose(gv[:, :7], (1, 0, 2)), gv[:, 8:]

    with jax.named_scope("coarse_up"):
        (c1,) = call(
            coarse_up, "coarse_up", [(4, 16, 128)],
            [
                vm(9, 16, 128), vm(9, 7, 16, 128), vm(7, 16, 128), vm(2, 3, 16, 256),
                vm(384, 128),
                vm(9, 24, 128), vm(9, 9, 24, 128), vm(7, 24, 128), vm(7, 24, 128),
                vm(12, 32, 128), vm(12, 32, 128), vm(3, 12, 32, 128), vm(12, 32, 128),
            ],
            pos, g3e, v2e, c3lo, c3own, c3hi, g2e, c2lo, c2own, c2hi, g1e, v1, v1lo, v1hi, cx, clo, chi,
        )

    with jax.named_scope("one_back"):
        c1e = wide(wide(c1, "gx", 0, 3), "gy", 1, 8)

    with jax.named_scope("fine_up"):
        (out,) = call(
            fine_up, "fine_up", [(8, 32, 256)],
            [vm(16, 48, 256)] * 2 + [vm(10, 48, 128)], pos, s0, w0, v0, c1e,
        )
    return out


def solution(mesh):
    in_specs = (
        P("gx", "gy", None),
        P("gx", "gy", None),
        P(None, "gx", "gy", None),
        P(None, "gx", "gy", None),
        P(None, "gx", "gy", None),
    )
    return jax.shard_map(
        on_device, mesh=mesh, in_specs=in_specs, out_specs=P("gx", "gy", None), check_vma=False
    )
```
